1024 devices in a mesh: row: 32 (over y, x_hi, core), col: 32 (over z, x_lo).
Axes of the slice: x: 8 (x_hi: 2, x_lo: 4; x = x_hi * 4 + x_lo), y: 8, z: 8, core: 2. Of those that a mesh axis runs over, the one named last changes fastest.
Arguments:
- tokens: bfloat16 [512, 8192], P('col', 'row'), may hold values from -6 to 6
- w_packed: bfloat16 [32, 32, 14, 128, 128], P('row', 'col'), may hold values from -0.09375 to 0.09375
- kept_rows: int32 [32, 32, 14], P('row', 'col'), may hold values from 0 to 1, as said below
- kept_cols: int32 [32, 32, 14], P('row', 'col'), may hold values from 0 to 6, as said below
- kept_count: int32 [32, 32], P('row', 'col'), may hold values from 1 to 14, as said below
- grad_act: bfloat16 [512, 28672], P('row', 'col'), may hold values from -6 to 6
Outputs:
- activation: bfloat16 [512, 28672], P('row', 'col')
- input_grad: bfloat16 [512, 8192], P('col', 'row')
- weight_grad: bfloat16 [32, 32, 14, 128, 128], P('row', 'col')
The draws below stay inside these ranges and needn't reach their ends.
Inputs may be any that keep to these rules, and one draw needn't show every extreme that they name: Within each tile, the 14 slots name every block of the tile once (kept_rows[r, c, s] * 7 + kept_cols[r, c, s] runs over all block places). `kept_cols`: see kept_rows. `kept_count`: some tile in every draw keeps all 14 blocks.
All inputs are finite; a program needn't handle non-finite values.
Results may differ from the reference program's by a relative error of at most 0.0049.
Values may be sent and summed in bfloat16 or wider, within the bound.
A program may use at most 32 MiB of HBM per device.

```python
import jax
import jax.numpy as jnp

D = 8192
FF = 28672
BLK = 128
TOKENS = 512
RB = 2
CB = 7
CAP = 14
N_ROW = 32
N_COL = 32


def kept_layout(key):
    tile_keys = jax.random.split(jax.random.fold_in(key, 11), N_ROW * N_COL)
    shuffled = jax.vmap(lambda one_key: jax.random.permutation(one_key, CAP))(tile_keys)
    return shuffled.reshape(N_ROW, N_COL, CAP).astype(jnp.int32)


def draw_kept_rows(key, part):
    return (kept_layout(key) // CB).astype(jnp.int32)


def draw_kept_cols(key, part):
    return (kept_layout(key) % CB).astype(jnp.int32)


def draw_kept_count(key, part):
    counts = jax.random.randint(jax.random.fold_in(key, 12), (N_ROW * N_COL,), 1, CAP + 1)
    fullest = jax.random.randint(jax.random.fold_in(key, 13), (), 0, N_ROW * N_COL)
    counts = jnp.where(jnp.arange(N_ROW * N_COL) == fullest, CAP, counts)
    return counts.reshape(N_ROW, N_COL).astype(jnp.int32)


def level_of(key, shape, cuts, smallest, largest):
    level = 1.0
    for axis_at, blocks in cuts:
        steps = jax.random.uniform(jax.random.fold_in(jax.random.fold_in(key, 6), axis_at), (blocks,), jnp.float32, smallest / len(cuts), largest / len(cuts))
        level = level * jnp.repeat(jnp.exp(steps), shape[axis_at] // blocks).reshape((-1,) + (1,) * (len(shape) - 1 - axis_at))
    return level


def noise(stream_key, extent, deviation, most, cuts=(), kind=jnp.bfloat16):
    array = deviation * jax.random.normal(stream_key, extent, jnp.float32)
    if cuts:
        array = array * level_of(stream_key, extent, cuts, -0.22, 0.18)
    return jnp.clip(array, -most, most).astype(kind)


def setup_inputs(seed: int = 0) -> dict:
    key_list = jax.random.split(jax.random.key(seed), 7)
    tokens = noise(key_list[0], (TOKENS, D), 1.0, 6.0, ((0, 32), (1, 32)))
    w_packed = noise(key_list[1], (N_ROW, N_COL, CAP, BLK, BLK), (D // 2) ** -0.5, 0.09375, ((0, 32), (1, 32)))
    kept_rows = draw_kept_rows(jax.random.fold_in(key_list[6], 71), 0)
    kept_cols = draw_kept_cols(jax.random.fold_in(key_list[6], 71), 0)
    kept_count = draw_kept_count(jax.random.fold_in(key_list[6], 71), 0)
    grad_act = noise(key_list[5], (TOKENS, FF), 1.0, 6.0, ((0, 32), (1, 32)))
    return dict(tokens=tokens, w_packed=w_packed, kept_rows=kept_rows, kept_cols=kept_cols, kept_count=kept_count, grad_act=grad_act)


gelu_scale = 0.7978845608
gelu_cubic = 0.044715


def dense_weight(w_packed, kept_rows, kept_cols, kept_count):
    live_slots = jnp.arange(CAP)[None, None, :] < kept_count[:, :, None]
    blocks = jnp.where(live_slots[..., None, None], w_packed, jnp.zeros_like(w_packed))
    places = (kept_rows * CB + kept_cols).astype(jnp.int32)
    row_index = jnp.broadcast_to(jnp.arange(N_ROW)[:, None, None], places.shape)
    col_index = jnp.broadcast_to(jnp.arange(N_COL)[None, :, None], places.shape)
    grid = jnp.zeros((N_ROW, N_COL, RB * CB, BLK, BLK), w_packed.dtype)
    grid = grid.at[row_index, col_index, places].set(blocks)
    grid = grid.reshape(N_ROW, N_COL, RB, CB, BLK, BLK).transpose(0, 2, 4, 1, 3, 5)
    return grid.reshape(D, FF), places, live_slots


def reference(tokens, w_packed, kept_rows, kept_cols, kept_count, grad_act):
    weight, places, live_slots = dense_weight(w_packed, kept_rows, kept_cols, kept_count)
    hidden = jnp.dot(tokens, weight, preferred_element_type=jnp.float32)
    inner = gelu_scale * (hidden + gelu_cubic * hidden * hidden * hidden)
    tangent = jnp.tanh(inner)
    activation = (0.5 * hidden * (1.0 + tangent)).astype(jnp.bfloat16)
    slope = 0.5 * (1.0 + tangent) + 0.5 * hidden * (1.0 - tangent * tangent) * gelu_scale * (1.0 + 3.0 * gelu_cubic * hidden * hidden)
    slope_grad = (grad_act.astype(jnp.float32) * slope).astype(jnp.bfloat16)
    input_grad = jnp.dot(slope_grad, weight.T, preferred_element_type=jnp.float32).astype(jnp.bfloat16)
    full_grad = jnp.dot(tokens.T, slope_grad, preferred_element_type=jnp.float32)
    tiles = full_grad.reshape(N_ROW, RB, BLK, N_COL, CB, BLK).transpose(0, 3, 1, 4, 2, 5)
    tiles = tiles.reshape(N_ROW, N_COL, RB * CB, BLK, BLK)
    picked = jnp.take_along_axis(tiles, places[..., None, None], axis=2)
    weight_grad = jnp.where(live_slots[..., None, None], picked, jnp.zeros_like(picked)).astype(jnp.bfloat16)
    return activation, input_grad, weight_grad
```

```python
import functools

import jax
import jax.numpy as jnp
from jax import lax
from jax.experimental import pallas as pl
from jax.experimental.pallas import tpu as pltpu
from jax.sharding import PartitionSpec as P

MESH = pl.DeviceIdType.MESH
BF16, F32 = jnp.bfloat16, jnp.float32

gelu_scale = 0.7978845608
gelu_cubic = 0.044715

X_LO = 4
X_HI = 2
CORES = 2


def gelu_pair(hidden, cotangent):
    inner = gelu_scale * (hidden + gelu_cubic * hidden * hidden * hidden)
    tangent = jnp.tanh(inner)
    activation = (0.5 * hidden * (1.0 + tangent)).astype(BF16)
    slope = 0.5 * (1.0 + tangent) + 0.5 * hidden * (1.0 - tangent * tangent) * gelu_scale * (
        1.0 + 3.0 * gelu_cubic * hidden * hidden
    )
    return activation, (cotangent.astype(F32) * slope).astype(BF16)


def kernel(
    ring, row_blocks, col_blocks,
    rows_ref, cols_ref, count_ref, tokens_ref, w_ref, gact_ref,
    act_ref, ig_ref, wg_ref,
    tok, dense, half_send, half_recv, half_own, y_send, y_recv, x_send, x_recv,
    gpair, acts, slope, g_full, z_send, z_recv, d_send, d_recv, wg_full,
    ssem, rsem, lsem,
):
    n = ring
    row, col = lax.axis_index("row"), lax.axis_index("col")
    core, x_hi, y = lax.rem(row, CORES), lax.rem(row // CORES, X_HI), row // (CORES * X_HI)
    x_lo, z = lax.rem(col, X_LO), col // X_LO
    slots = w_ref.shape[2]
    block = w_ref.shape[3]
    width, hidden_width = row_blocks * block, col_blocks * block
    slab = tokens_ref.shape[0]
    pair = X_HI * slab

    def at_y(other):
        return ((other * X_HI + x_hi) * CORES + core, col)

    def at_z(other):
        return (row, other * X_LO + x_lo)

    def at_x(other):
        return (row, z * X_LO + other)

    sibling = ((y * X_HI + x_hi) * CORES + 1 - core, col)
    partner = ((y * X_HI + 1 - x_hi) * CORES + core, col)

    def turn(base, step, size):
        return lax.rem(base + step + size, size)

    barrier = pltpu.get_barrier_semaphore()
    peers = [sibling, partner]
    peers += [at_x(turn(x_lo, e, X_LO)) for e in range(1, X_LO)]
    peers += [at_z(turn(z, e, n)) for e in range(1, n)]
    peers += [at_y(turn(y, e, n)) for e in range(1, n)]
    for peer in peers:
        pl.semaphore_signal(barrier, inc=1, device_id=peer, device_id_type=MESH)

    used = [0]

    def numbers(size):
        used[0] += size
        return used[0] - size

    def remote(src, dst, index, peer):
        return pltpu.make_async_remote_copy(
            src_ref=src, dst_ref=dst, send_sem=ssem.at[index], recv_sem=rsem.at[index],
            device_id=peer, device_id_type=MESH,
        )

    my_core, my_pair = lax.rem(x_lo, CORES), x_lo // CORES
    local = [
        pltpu.make_async_copy(tokens_ref, tok.at[z, my_core, my_pair], lsem.at[0]),
        pltpu.make_async_copy(gact_ref, gpair.at[x_hi], lsem.at[1]),
    ]
    for copy in local:
        copy.start()
    pl.semaphore_wait(barrier, len(peers))

    sends = []
    ax = numbers(X_LO)
    for e in range(1, X_LO):
        copy = remote(tokens_ref, tok.at[z, my_core, my_pair], ax + e, at_x(turn(x_lo, e, X_LO)))
        copy.start()
        sends.append(copy)
    gp = numbers(1)
    gp_copy = remote(gact_ref, gpair.at[x_hi], gp, partner)
    gp_copy.start()
    sends.append(gp_copy)

    count = count_ref[0, 0]
    places = [rows_ref[0, 0, s] * col_blocks + cols_ref[0, 0, s] for s in range(slots)]
    for p in range(row_blocks * col_blocks):
        slot = jnp.int32(0)
        for s in range(slots):
            slot = jnp.where(places[s] == p, s, slot)
        live = jnp.where(slot < count, 1, 0).astype(F32)
        r, c = p // col_blocks, p % col_blocks
        dense[r * block:(r + 1) * block, c * block:(c + 1) * block] = (
            w_ref[0, 0, slot].astype(F32) * live
        ).astype(BF16)

    for copy in local:
        copy.wait()
    for e in range(1, X_LO):
        source = turn(x_lo, -e, X_LO)
        remote(
            tokens_ref, tok.at[z, lax.rem(source, CORES), source // CORES], ax + e,
            at_x(turn(x_lo, e, X_LO)),
        ).wait_recv()
    far_first = sorted(range(1, n), key=lambda d: (-min(d, n - d), d))
    near_first = far_first[::-1]
    az = numbers(n)
    for d in far_first:
        copy = remote(tok.at[z], tok.at[z], az + d, at_z(turn(z, d, n)))
        copy.start()
        sends.append(copy)
    for d in near_first:
        source = turn(z, -d, n)
        remote(tok.at[source], tok.at[source], az + d, at_z(turn(z, d, n))).wait_recv()

    order = far_first + [0]
    b1 = numbers(2)
    cuts = [(0, n // 2), (n // 2, n)]
    b1_copies = []

    def product(which, low, high):
        lhs = jnp.concatenate(
            [tok[turn(y, d, n), which].reshape(pair, width) for d in order[low:high]], axis=0
        )
        return jnp.dot(lhs, dense[...], preferred_element_type=F32).reshape(
            high - low, pair, hidden_width
        )

    for i, (low, high) in enumerate(cuts):
        half_send[low:high] = product(1 - core, low, high)
        copy = remote(half_send.at[pl.ds(low, high - low)], half_recv.at[pl.ds(low, high - low)], b1 + i, sibling)
        copy.start()
        b1_copies.append(copy)
        sends.append(copy)
    for low, high in cuts:
        half_own[low:high] = product(core, low, high)
    b2 = numbers(n)
    y_copies = {}
    for i, (low, high) in enumerate(cuts):
        b1_copies[i].wait_recv()
        for at in range(low, high):
            d = order[at]
            if d:
                y_send[at] = (half_own[at] + half_recv[at]).astype(BF16)
                y_copies[d] = remote(y_send.at[at], y_recv.at[d], b2 + d, at_y(turn(y, d, n)))
                y_copies[d].start()
                sends.append(y_copies[d])
    total = half_own[n - 1] + half_recv[n - 1]
    for d in near_first:
        y_copies[d].wait_recv()
        total = total + y_recv[d].astype(F32)
    b3 = numbers(1)
    x_send[...] = total.astype(BF16)
    x_copy = remote(x_send, x_recv, b3, partner)
    x_copy.start()
    sends.append(x_copy)
    half_own[0] = total
    x_copy.wait_recv()
    gp_copy.wait_recv()
    hidden = half_own[0] + x_recv[...].astype(F32)
    activation, grad = gelu_pair(hidden, gpair[...].reshape(pair, hidden_width))
    acts[...] = activation.reshape(X_HI, slab, hidden_width)
    slope[y, core] = grad.reshape(X_HI, slab, hidden_width)

    c2, c3 = numbers(n), numbers(n)
    for d in far_first:
        copy = remote(slope.at[y, core], slope.at[y, core], c2 + d, at_y(turn(y, d, n)))
        copy.start()
        sends.append(copy)
    copy = remote(slope.at[y, core], slope.at[y, core], c3, sibling)
    copy.start()
    sends.append(copy)
    act_ref[...] = acts[x_hi]

    d1 = numbers(n)

    def to_z(to):
        return pltpu.make_async_remote_copy(
            src_ref=z_send.at[to], dst_ref=z_recv.at[z], send_sem=ssem.at[d1 + to],
            recv_sem=rsem.at[d1 + z], device_id=at_z(to), device_id_type=MESH,
        )

    def input_part(d):
        source = turn(y, -d, n)
        remote(slope.at[source, 1 - core], slope.at[source, 1 - core], c3 + d, sibling).wait_recv()
        lhs = slope[source].reshape(CORES * pair, hidden_width)
        part = lax.dot_general(
            lhs, dense[...], (((1,), (1,)), ((), ())), preferred_element_type=F32
        )
        g_full[source] = part
        z_send[source] = part.astype(BF16).reshape(CORES * pair, width)

        @pl.when(source != z)
        def _():
            to_z(source).start()

    waiting = [0]
    for d in near_first:
        source = turn(y, -d, n)
        remote(slope.at[source, core], slope.at[source, core], c2 + d, at_y(turn(y, d, n))).wait_recv()
        copy = remote(slope.at[source, core], slope.at[source, core], c3 + d, sibling)
        copy.start()
        sends.append(copy)
        input_part(waiting[0])
        waiting[0] = d
    input_part(waiting[0])

    all_tokens = tok[...].reshape(n * CORES * pair, width)
    all_slopes = slope[...].reshape(n * CORES * pair, hidden_width)
    full = lax.dot_general(
        all_tokens, all_slopes, (((0,), (0,)), ((), ())), preferred_element_type=F32
    )
    for p in range(row_blocks * col_blocks):
        r, c = p // col_blocks, p % col_blocks
        wg_full[p] = full[r * block:(r + 1) * block, c * block:(c + 1) * block]
    for s in range(slots):
        live = jnp.where(s < count, 1, 0).astype(F32)
        wg_ref[0, 0, s] = (wg_full[places[s]] * live).astype(BF16)

    total = g_full[z]
    for e in near_first:
        source = turn(z, -e, n)
        pltpu.make_async_remote_copy(
            src_ref=z_send.at[source], dst_ref=z_recv.at[source], send_sem=ssem.at[d1 + source],
            recv_sem=rsem.at[d1 + source], device_id=at_z(source), device_id_type=MESH,
        ).wait_recv()
        total = total + z_recv[source].astype(F32)
    d_send[...] = total.reshape(CORES, X_HI, slab, width)
    d2 = numbers(X_LO)
    d_copies = []
    for e in range(1, X_LO):
        to = turn(x_lo, e, X_LO)
        copy = remote(d_send.at[lax.rem(to, CORES), to // CORES], d_recv.at[e], d2 + e, at_x(to))
        copy.start()
        d_copies.append(copy)
        sends.append(copy)
    result = d_send[my_core, my_pair]
    for e in range(1, X_LO):
        d_copies[e - 1].wait_recv()
        result = result + d_recv[e]
    ig_ref[...] = result.astype(BF16)

    for copy in sends:
        copy.wait_send()
    for e in range(1, n):
        to_z(turn(z, e, n)).wait_send()


def on_device(ring, tokens, w_packed, kept_rows, kept_cols, kept_count, grad_act):
    n = ring
    block, slots = w_packed.shape[-1], w_packed.shape[2]
    slab, width = tokens.shape
    hidden_width = grad_act.shape[1]
    row_blocks, col_blocks = width // block, hidden_width // block
    pair = X_HI * slab
    sems = 3 * X_LO + 2 + 2 + 6 * n
    vmem, smem = pl.BlockSpec(memory_space=pltpu.VMEM), pl.BlockSpec(memory_space=pltpu.SMEM)
    return tuple(pl.pallas_call(
        functools.partial(kernel, n, row_blocks, col_blocks),
        out_shape=(
            jax.ShapeDtypeStruct(grad_act.shape, BF16),
            jax.ShapeDtypeStruct(tokens.shape, BF16),
            jax.ShapeDtypeStruct(w_packed.shape, BF16),
        ),
        in_specs=[smem, smem, smem, vmem, vmem, vmem],
        out_specs=(vmem, vmem, vmem),
        scratch_shapes=[
            pltpu.VMEM((n, CORES, X_HI, slab, width), BF16),
            pltpu.VMEM((width, hidden_width), BF16),
            pltpu.VMEM((n, pair, hidden_width), F32),
            pltpu.VMEM((n, pair, hidden_width), F32),
            pltpu.VMEM((n, pair, hidden_width), F32),
            pltpu.VMEM((n, pair, hidden_width), BF16),
            pltpu.VMEM((n, pair, hidden_width), BF16),
            pltpu.VMEM((pair, hidden_width), BF16),
            pltpu.VMEM((pair, hidden_width), BF16),
            pltpu.VMEM((X_HI, slab, hidden_width), BF16),
            pltpu.VMEM((X_HI, slab, hidden_width), BF16),
            pltpu.VMEM((n, CORES, X_HI, slab, hidden_width), BF16),
            pltpu.VMEM((n, CORES * pair, width), F32),
            pltpu.VMEM((n, CORES * pair, width), BF16),
            pltpu.VMEM((n, CORES * pair, width), BF16),
            pltpu.VMEM((CORES, X_HI, slab, width), F32),
            pltpu.VMEM((X_LO, slab, width), F32),
            pltpu.VMEM((row_blocks * col_blocks, block, block), F32),
            pltpu.SemaphoreType.DMA((sems,)),
            pltpu.SemaphoreType.DMA((sems,)),
            pltpu.SemaphoreType.DMA((2,)),
        ],
        compiler_params=pltpu.CompilerParams(collective_id=0, has_side_effects=True),
    )(kept_rows, kept_cols, kept_count, tokens, w_packed, grad_act))


def solution(mesh):
    ring = mesh.shape["row"] // (CORES * X_HI)
    placed = (
        P("col", "row"),
        P("row", "col", None, None, None),
        P("row", "col", None),
        P("row", "col", None),
        P("row", "col"),
        P("row", "col"),
    )
    return jax.shard_map(
        functools.partial(on_device, ring),
        mesh=mesh,
        in_specs=placed,
        out_specs=(P("row", "col"), P("col", "row"), P("row", "col", None, None, None)),
        check_vma=False,
    )
```

```python
import functools

import jax
import jax.numpy as jnp
from jax import lax
from jax.experimental import pallas as pl
from jax.experimental.pallas import tpu as pltpu
from jax.sharding import PartitionSpec as P

MESH = pl.DeviceIdType.MESH
BF16, F32 = jnp.bfloat16, jnp.float32

gelu_scale = 0.7978845608
gelu_cubic = 0.044715

X_LO = 4
X_HI = 2
CORES = 2


def gelu_pair(hidden, cotangent):
    inner = gelu_scale * (hidden + gelu_cubic * hidden * hidden * hidden)
    tangent = jnp.tanh(inner)
    activation = (0.5 * hidden * (1.0 + tangent)).astype(BF16)
    slope = 0.5 * (1.0 + tangent) + 0.5 * hidden * (1.0 - tangent * tangent) * gelu_scale * (
        1.0 + 3.0 * gelu_cubic * hidden * hidden
    )
    return activation, (cotangent.astype(F32) * slope).astype(BF16)


def kernel(
    ring, row_blocks, col_blocks, cuts,
    rows_ref, cols_ref, count_hbm, tokens_ref, w_hbm, gact_ref,
    act_ref, ig_ref, wg_ref,
    tok, dense, w_ref, gpair, acts, g_full, z_send, z_recv, d_send, d_recv, wg_full, count_ref,
    ssem, rsem, lsem, *per_cut,
):
    n = ring
    part, sib, own, y_send, y_recv, x_send, x_recv, slope = (
        per_cut[i * len(cuts):(i + 1) * len(cuts)] for i in range(8)
    )
    row, col = lax.axis_index("row"), lax.axis_index("col")
    core, x_hi, y = lax.rem(row, CORES), lax.rem(row // CORES, X_HI), row // (CORES * X_HI)
    x_lo, z = lax.rem(col, X_LO), col // X_LO
    slots, block = w_ref.shape[0], w_ref.shape[1]
    width = row_blocks * block
    slab = tokens_ref.shape[0]
    pair = X_HI * slab

    def at_y(other):
        return ((other * X_HI + x_hi) * CORES + core, col)

    def at_z(other):
        return (row, other * X_LO + x_lo)

    def at_x(other):
        return (row, z * X_LO + other)

    sibling = ((y * X_HI + x_hi) * CORES + 1 - core, col)
    partner = ((y * X_HI + 1 - x_hi) * CORES + core, col)

    def turn(base, step, size):
        return lax.rem(base + step + size, size)

    barrier = pltpu.get_barrier_semaphore()
    peers = [sibling, partner]
    peers += [at_x(turn(x_lo, e, X_LO)) for e in range(1, X_LO)]
    peers += [at_z(turn(z, e, n)) for e in range(1, n)]
    peers += [at_y(turn(y, e, n)) for e in range(1, n)]
    for peer in peers:
        pl.semaphore_signal(barrier, inc=1, device_id=peer, device_id_type=MESH)

    used = [0]

    def numbers(size):
        used[0] += size
        return used[0] - size

    def remote(src, dst, send, receive, peer):
        return pltpu.make_async_remote_copy(
            src_ref=src, dst_ref=dst, send_sem=ssem.at[send], recv_sem=rsem.at[receive],
            device_id=peer, device_id_type=MESH,
        )

    steps = [i // 2 + (i % 2) * (n // 2) for i in range(n)]

    def piece(o):
        return lax.rem(y + z + o, n)

    def y_other(o):
        return lax.rem(y - z - o + 2 * n, n)

    def z_other(o):
        return lax.rem(z - y - o + 2 * n, n)

    my_core, my_pair = lax.rem(x_lo, CORES), x_lo // CORES
    mine = tok.at[z, my_core, my_pair]
    local = [
        pltpu.make_async_copy(tokens_ref, mine, lsem.at[0]),
        pltpu.make_async_copy(w_hbm.at[0, 0], w_ref, lsem.at[1]),
        pltpu.make_async_copy(count_hbm, count_ref, lsem.at[2]),
        pltpu.make_async_copy(gact_ref, gpair.at[x_hi], lsem.at[3]),
    ]
    for copy in local:
        copy.start()
    local[0].wait()
    pl.semaphore_wait(barrier, len(peers))

    sends = []
    ax = numbers(X_LO)
    for e in range(1, X_LO):
        copy = remote(mine, mine, ax + e, ax + e, at_x(turn(x_lo, e, X_LO)))
        copy.start()
        sends.append(copy)

    for copy in local[1:]:
        copy.wait()
    gp = numbers(1)
    gp_copy = remote(gpair.at[x_hi], gpair.at[x_hi], gp, gp, partner)
    gp_copy.start()
    sends.append(gp_copy)
    count = count_ref[0, 0]
    places = [rows_ref[0, 0, s] * col_blocks + cols_ref[0, 0, s] for s in range(slots)]
    for p in range(row_blocks * col_blocks):
        slot = jnp.int32(0)
        for s in range(slots):
            slot = jnp.where(places[s] == p, s, slot)
        live = jnp.where(slot < count, 1, 0).astype(F32)
        r, c = p // col_blocks, p % col_blocks
        dense[r * block:(r + 1) * block, c * block:(c + 1) * block] = (
            w_ref[slot].astype(F32) * live
        ).astype(BF16)

    for e in range(1, X_LO):
        source = turn(x_lo, -e, X_LO)
        theirs = tok.at[z, lax.rem(source, CORES), source // CORES]
        remote(theirs, theirs, ax + e, ax + e, at_x(source)).wait_recv()
    az = numbers(n)
    for o in steps:
        to = z_other(o)

        @pl.when(to != z)
        def _():
            remote(tok.at[z], tok.at[z], az + to, az + z, at_z(to)).start()

    b1 = [numbers(n) for _ in cuts]
    b2 = [numbers(n) for _ in cuts]
    b3 = [numbers(1) for _ in cuts]
    c2 = [numbers(n) for _ in cuts]
    c3 = [numbers(n) for _ in cuts]
    d1, d2 = numbers(n), numbers(X_LO)

    def half_copy(h, i):
        return remote(part[h].at[i, 1 - core], sib[h].at[i], b1[h] + i, b1[h] + i, sibling)

    def y_copy(h, i, to):
        return remote(y_send[h].at[i], y_recv[h].at[y], b2[h] + to, b2[h] + y, at_y(to))

    def multiply(h, i):
        low, high = cuts[h]
        j = piece(steps[i])
        if h == 0:
            @pl.when(j != z)
            def _():
                remote(tok.at[j], tok.at[j], az + j, az + j, at_z(j)).wait_recv()
        product = jnp.dot(
            tok[j].reshape(CORES * pair, width), dense[:, low:high], preferred_element_type=F32
        )
        part[h][i] = product.reshape(CORES, pair, high - low)
        half_copy(h, i).start()

    def pass_on(h, i):
        j = piece(steps[i])
        half_copy(h, i).wait_recv()
        both = part[h][i, core] + sib[h][i]
        y_send[h][i] = both.astype(BF16)

        @pl.when(j == y)
        def _():
            own[h][...] = both

        @pl.when(j != y)
        def _():
            y_copy(h, i, j).start()

    before = None
    for h in range(len(cuts)):
        for i in range(n):
            multiply(h, i)
            if before is not None:
                pass_on(*before)
            before = (h, i)
    pass_on(*before)

    for h, (low, high) in enumerate(cuts):
        for o in steps:
            source = y_other(o)

            @pl.when(source != y)
            def _():
                remote(
                    y_send[h].at[0], y_recv[h].at[source], b2[h] + source, b2[h] + source, at_y(source)
                ).wait_recv()
                own[h][...] += y_recv[h][source].astype(F32)

        x_send[h][...] = own[h][...].astype(BF16)
        x_copy = remote(x_send[h], x_recv[h], b3[h], b3[h], partner)
        x_copy.start()
        sends.append(x_copy)
        x_copy.wait_recv()
        if h == 0:
            gp_copy.wait_recv()
        hidden = own[h][...] + x_recv[h][...].astype(F32)
        activation, grad = gelu_pair(hidden, gpair[:, :, low:high].reshape(pair, high - low))
        acts[:, :, low:high] = activation.reshape(X_HI, slab, high - low)
        slope[h][y, core] = grad.reshape(X_HI, slab, high - low)

        for o in steps:
            to = y_other(o)

            @pl.when(to != y)
            def _():
                here = slope[h].at[y, core]
                remote(here, here, c2[h] + to, c2[h] + y, at_y(to)).start()

        here = slope[h].at[y, core]
        remote(here, here, c3[h] + y, c3[h] + y, sibling).start()
    act_ref[...] = acts[x_hi]

    def z_copy(to):
        return remote(z_send.at[to], z_recv.at[z], d1 + to, d1 + z, at_z(to))

    def relay(h, i):
        j = piece(steps[i])

        @pl.when(j != y)
        def _():
            there = slope[h].at[j, core]
            remote(there, there, c2[h] + j, c2[h] + j, at_y(j)).wait_recv()
            remote(there, there, c3[h] + j, c3[h] + j, sibling).start()

    def input_part(h, i):
        low, high = cuts[h]
        j = piece(steps[i])
        there = slope[h].at[j, 1 - core]
        remote(there, there, c3[h] + j, c3[h] + j, sibling).wait_recv()
        share = lax.dot_general(
            slope[h][j].reshape(CORES * pair, high - low), dense[:, low:high],
            (((1,), (1,)), ((), ())), preferred_element_type=F32,
        )
        if h:
            share = share + g_full[j]
        g_full[j] = share
        if h == len(cuts) - 1:
            z_send[j] = share.astype(BF16)

            @pl.when(j != z)
            def _():
                z_copy(j).start()

    before = None
    for h in range(len(cuts)):
        for i in range(n):
            relay(h, i)
            if before is not None:
                input_part(*before)
            before = (h, i)
    input_part(*before)

    all_tokens = tok[...].reshape(n * CORES * pair, width)
    for h, (low, high) in enumerate(cuts):
        full = lax.dot_general(
            all_tokens, slope[h][...].reshape(n * CORES * pair, high - low),
            (((0,), (0,)), ((), ())), preferred_element_type=F32,
        )
        for r in range(row_blocks):
            for c in range(low // block, high // block):
                wg_full[r * col_blocks + c] = full[
                    r * block:(r + 1) * block, c * block - low:(c + 1) * block - low
                ]
    for s in range(slots):
        live = jnp.where(s < count, 1, 0).astype(F32)
        wg_ref[0, 0, s] = (wg_full[places[s]] * live).astype(BF16)

    d_send[...] = g_full[z].reshape(CORES, X_HI, slab, width)
    for o in steps:
        source = z_other(o)

        @pl.when(source != z)
        def _():
            remote(z_send.at[0], z_recv.at[source], d1 + source, d1 + source, at_z(source)).wait_recv()
            d_send[...] += z_recv[source].astype(F32).reshape(CORES, X_HI, slab, width)

    d_copies = []
    for e in range(1, X_LO):
        to = turn(x_lo, e, X_LO)
        copy = remote(d_send.at[lax.rem(to, CORES), to // CORES], d_recv.at[e], d2 + e, d2 + e, at_x(to))
        copy.start()
        d_copies.append(copy)
        sends.append(copy)
    result = d_send[my_core, my_pair]
    for e in range(1, X_LO):
        d_copies[e - 1].wait_recv()
        result = result + d_recv[e]
    ig_ref[...] = result.astype(BF16)

    for copy in sends:
        copy.wait_send()
    for e in range(1, n):
        to = turn(z, e, n)
        remote(tok.at[z], tok.at[z], az + to, az + z, at_z(to)).wait_send()
        z_copy(to).wait_send()
        to = turn(y, e, n)
        for h in range(len(cuts)):
            y_copy(h, 0, to).wait_send()
            here = slope[h].at[y, core]
            remote(here, here, c2[h] + to, c2[h] + y, at_y(to)).wait_send()
    for h in range(len(cuts)):
        for i in range(n):
            half_copy(h, i).wait_send()
            there = slope[h].at[i, core]
            remote(there, there, c3[h] + i, c3[h] + i, sibling).wait_send()


def on_device(ring, tokens, w_packed, kept_rows, kept_cols, kept_count, grad_act):
    n = ring
    block, slots = w_packed.shape[-1], w_packed.shape[2]
    slab, width = tokens.shape
    hidden_width = grad_act.shape[1]
    row_blocks, col_blocks = width // block, hidden_width // block
    pair = X_HI * slab
    middle = (col_blocks + 1) // 2 * block
    cuts = ((0, middle), (middle, hidden_width))
    sems = 2 * X_LO + 1 + 2 * n + len(cuts) * (4 * n + 1)
    vmem, smem = pl.BlockSpec(memory_space=pltpu.VMEM), pl.BlockSpec(memory_space=pltpu.SMEM)
    hbm = pl.BlockSpec(memory_space=pltpu.HBM)

    def each(lead, kind):
        return [pltpu.VMEM(lead + (high - low,), kind) for low, high in cuts]

    return tuple(pl.pallas_call(
        functools.partial(kernel, n, row_blocks, col_blocks, cuts),
        out_shape=(
            jax.ShapeDtypeStruct(grad_act.shape, BF16),
            jax.ShapeDtypeStruct(tokens.shape, BF16),
            jax.ShapeDtypeStruct(w_packed.shape, BF16),
        ),
        in_specs=[smem, smem, hbm, hbm, hbm, hbm],
        out_specs=(vmem, vmem, vmem),
        scratch_shapes=[
            pltpu.VMEM((n, CORES, X_HI, slab, width), BF16),
            pltpu.VMEM((width, hidden_width), BF16),
            pltpu.VMEM((slots, block, block), BF16),
            pltpu.VMEM((X_HI, slab, hidden_width), BF16),
            pltpu.VMEM((X_HI, slab, hidden_width), BF16),
            pltpu.VMEM((n, CORES * pair, width), F32),
            pltpu.VMEM((n, CORES * pair, width), BF16),
            pltpu.VMEM((n, CORES * pair, width), BF16),
            pltpu.VMEM((CORES, X_HI, slab, width), F32),
            pltpu.VMEM((X_LO, slab, width), F32),
            pltpu.VMEM((row_blocks * col_blocks, block, block), F32),
            pltpu.SMEM((1, 1), jnp.int32),
            pltpu.SemaphoreType.DMA((sems,)),
            pltpu.SemaphoreType.DMA((sems,)),
            pltpu.SemaphoreType.DMA((4,)),
            *each((n, CORES, pair), F32),
            *each((n, pair), F32),
            *each((pair,), F32),
            *each((n, pair), BF16),
            *each((n, pair), BF16),
            *each((pair,), BF16),
            *each((pair,), BF16),
            *each((n, CORES, X_HI, slab), BF16),
        ],
        compiler_params=pltpu.CompilerParams(
            collective_id=0, has_side_effects=True, vmem_limit_bytes=24 << 20
        ),
    )(kept_rows, kept_cols, kept_count, tokens, w_packed, grad_act))


def solution(mesh):
    ring = mesh.shape["row"] // (CORES * X_HI)
    placed = (
        P("col", "row"),
        P("row", "col", None, None, None),
        P("row", "col", None),
        P("row", "col", None),
        P("row", "col"),
        P("row", "col"),
    )
    return jax.shard_map(
        functools.partial(on_device, ring),
        mesh=mesh,
        in_specs=placed,
        out_specs=(P("row", "col"), P("col", "row"), P("row", "col", None, None, None)),
        check_vma=False,
    )
```

```python
import functools

import jax
import jax.numpy as jnp
from jax import lax
from jax.experimental import pallas as pl
from jax.experimental.pallas import tpu as pltpu
from jax.sharding import PartitionSpec as P

MESH = pl.DeviceIdType.MESH
BF16, F32 = jnp.bfloat16, jnp.float32

gelu_scale = 0.7978845608
gelu_cubic = 0.044715

X_LO = 4
X_HI = 2
CORES = 2


def gelu_pair(hidden, cotangent):
    inner = gelu_scale * (hidden + gelu_cubic * hidden * hidden * hidden)
    tangent = jnp.tanh(inner)
    activation = (0.5 * hidden * (1.0 + tangent)).astype(BF16)
    slope = 0.5 * (1.0 + tangent) + 0.5 * hidden * (1.0 - tangent * tangent) * gelu_scale * (
        1.0 + 3.0 * gelu_cubic * hidden * hidden
    )
    return activation, (cotangent.astype(F32) * slope).astype(BF16)


def kernel(
    ring, row_blocks, col_blocks, cuts,
    rows_ref, cols_ref, count_hbm, tokens_ref, w_hbm, gact_ref,
    act_ref, ig_ref, wg_ref,
    tok, dense, dense_t, w_ref, gpair, acts, g_full, z_send, z_recv, d_send, d_recv, wg_full, w_grad, in_grad, count_ref,
    ssem, rsem, lsem, *per_cut,
):
    n = ring
    part, sib, own, y_send, y_recv, x_send, x_recv, slope = (
        per_cut[i * len(cuts):(i + 1) * len(cuts)] for i in range(8)
    )
    row, col = lax.axis_index("row"), lax.axis_index("col")
    core, x_hi, y = lax.rem(row, CORES), lax.rem(row // CORES, X_HI), row // (CORES * X_HI)
    x_lo, z = lax.rem(col, X_LO), col // X_LO
    slots, block = w_ref.shape[0], w_ref.shape[1]
    width = row_blocks * block
    slab = tokens_ref.shape[0]
    pair = X_HI * slab

    def at_y(other):
        return ((other * X_HI + x_hi) * CORES + core, col)

    def at_z(other):
        return (row, other * X_LO + x_lo)

    def at_x(other):
        return (row, z * X_LO + other)

    sibling = ((y * X_HI + x_hi) * CORES + 1 - core, col)
    partner = ((y * X_HI + 1 - x_hi) * CORES + core, col)

    def turn(base, step, size):
        return lax.rem(base + step + size, size)

    barrier = pltpu.get_barrier_semaphore()
    peers = [sibling, partner]
    peers += [at_x(turn(x_lo, e, X_LO)) for e in range(1, X_LO)]
    peers += [at_z(turn(z, e, n)) for e in range(1, n)]
    peers += [at_y(turn(y, e, n)) for e in range(1, n)]
    for peer in peers:
        pl.semaphore_signal(barrier, inc=1, device_id=peer, device_id_type=MESH)

    used = [0]

    def numbers(size):
        used[0] += size
        return used[0] - size

    def remote(src, dst, send, receive, peer):
        return pltpu.make_async_remote_copy(
            src_ref=src, dst_ref=dst, send_sem=ssem.at[send], recv_sem=rsem.at[receive],
            device_id=peer, device_id_type=MESH,
        )

    steps = [i // 2 + (i % 2) * (n // 2) for i in range(n)]

    def piece(o):
        return lax.rem(y + z + o, n)

    def y_other(o):
        return lax.rem(y - z - o + 2 * n, n)

    def z_other(o):
        return lax.rem(z - y - o + 2 * n, n)

    my_core, my_pair = lax.rem(x_lo, CORES), x_lo // CORES
    mine = tok.at[z, my_core, my_pair]
    local = [
        pltpu.make_async_copy(tokens_ref, mine, lsem.at[0]),
        pltpu.make_async_copy(w_hbm.at[0, 0], w_ref, lsem.at[1]),
        pltpu.make_async_copy(count_hbm, count_ref, lsem.at[2]),
        pltpu.make_async_copy(gact_ref, gpair.at[x_hi], lsem.at[3]),
    ]
    for copy in local:
        copy.start()
    local[0].wait()
    pl.semaphore_wait(barrier, len(peers))

    sends = []
    ax = numbers(X_LO)
    for e in range(1, X_LO):
        copy = remote(mine, mine, ax + e, ax + e, at_x(turn(x_lo, e, X_LO)))
        copy.start()
        sends.append(copy)

    for copy in local[1:]:
        copy.wait()
    gp = numbers(1)
    gp_copy = remote(gpair.at[x_hi], gpair.at[x_hi], gp, gp, partner)
    gp_copy.start()
    sends.append(gp_copy)
    count = count_ref[0, 0]
    places = [rows_ref[0, 0, s] * col_blocks + cols_ref[0, 0, s] for s in range(slots)]
    for p in range(row_blocks * col_blocks):
        slot = jnp.int32(0)
        for s in range(slots):
            slot = jnp.where(places[s] == p, s, slot)
        live = jnp.where(slot < count, 1, 0).astype(F32)
        r, c = p // col_blocks, p % col_blocks
        dense[r * block:(r + 1) * block, c * block:(c + 1) * block] = (
            w_ref[slot].astype(F32) * live
        ).astype(BF16)
        dense_t[c * block:(c + 1) * block, r * block:(r + 1) * block] = jnp.transpose(
            w_ref[slot].astype(F32) * live
        ).astype(BF16)

    for e in range(1, X_LO):
        source = turn(x_lo, -e, X_LO)
        theirs = tok.at[z, lax.rem(source, CORES), source // CORES]
        remote(theirs, theirs, ax + e, ax + e, at_x(source)).wait_recv()
    az = numbers(n)
    for o in steps:
        to = z_other(o)

        @pl.when(to != z)
        def _():
            remote(tok.at[z], tok.at[z], az + to, az + z, at_z(to)).start()

    b1 = [numbers(n) for _ in cuts]
    b2 = [numbers(n) for _ in cuts]
    b3 = [numbers(1) for _ in cuts]
    c2 = [numbers(n) for _ in cuts]
    c3 = [numbers(n) for _ in cuts]
    d1, d2 = numbers(n), numbers(X_LO)

    def half_copy(h, i):
        return remote(part[h].at[i, 1 - core], sib[h].at[i], b1[h] + i, b1[h] + i, sibling)

    def y_copy(h, i, to):
        return remote(y_send[h].at[i], y_recv[h].at[y], b2[h] + to, b2[h] + y, at_y(to))

    def multiply(h, i):
        low, high = cuts[h]
        j = piece(steps[i])
        if h == 0:
            @pl.when(j != z)
            def _():
                remote(tok.at[j], tok.at[j], az + j, az + j, at_z(j)).wait_recv()
        product = jnp.dot(
            tok[j].reshape(CORES * pair, width), dense[:, low:high], preferred_element_type=F32
        )
        part[h][i] = product.reshape(CORES, pair, high - low)
        half_copy(h, i).start()

    def pass_on(h, i):
        j = piece(steps[i])
        half_copy(h, i).wait_recv()
        both = part[h][i, core] + sib[h][i]
        y_send[h][i] = both.astype(BF16)

        @pl.when(j == y)
        def _():
            own[h][...] = both

        @pl.when(j != y)
        def _():
            y_copy(h, i, j).start()

    before = None
    for h in range(len(cuts)):
        for i in range(n):
            multiply(h, i)
            if before is not None:
                pass_on(*before)
            before = (h, i)
    pass_on(*before)

    for h, (low, high) in enumerate(cuts):
        for o in steps:
            source = y_other(o)

            @pl.when(source != y)
            def _():
                remote(
                    y_send[h].at[0], y_recv[h].at[source], b2[h] + source, b2[h] + source, at_y(source)
                ).wait_recv()
                own[h][...] += y_recv[h][source].astype(F32)

        x_send[h][...] = own[h][...].astype(BF16)
        x_copy = remote(x_send[h], x_recv[h], b3[h], b3[h], partner)
        x_copy.start()
        sends.append(x_copy)
        x_copy.wait_recv()
        if h == 0:
            gp_copy.wait_recv()
        hidden = own[h][...] + x_recv[h][...].astype(F32)
        activation, grad = gelu_pair(hidden, gpair[:, :, low:high].reshape(pair, high - low))
        acts[:, :, low:high] = activation.reshape(X_HI, slab, high - low)
        slope[h][y, core] = grad.reshape(X_HI, slab, high - low)

        for o in steps:
            to = y_other(o)

            @pl.when(to != y)
            def _():
                here = slope[h].at[y, core]
                remote(here, here, c2[h] + to, c2[h] + y, at_y(to)).start()

        here = slope[h].at[y, core]
        remote(here, here, c3[h] + y, c3[h] + y, sibling).start()
    out_act = pltpu.make_async_copy(acts.at[x_hi], act_ref, lsem.at[4])
    out_act.start()

    def z_copy(to):
        return remote(z_send.at[to], z_recv.at[z], d1 + to, d1 + z, at_z(to))

    near_first = sorted(range(n), key=lambda d: (min(d, n - d), d))

    def arrival(h, i):
        return turn(y, -near_first[i], n)

    def relay(h, i):
        j = arrival(h, i)

        @pl.when(j != y)
        def _():
            there = slope[h].at[j, core]
            remote(there, there, c2[h] + j, c2[h] + j, at_y(j)).wait_recv()
            remote(there, there, c3[h] + j, c3[h] + j, sibling).start()

    def input_part(h, i):
        low, high = cuts[h]
        j = arrival(h, i)
        there = slope[h].at[j, 1 - core]
        remote(there, there, c3[h] + j, c3[h] + j, sibling).wait_recv()
        share = jnp.dot(
            slope[h][j].reshape(CORES * pair, high - low), dense_t[low:high], preferred_element_type=F32
        )
        if h:
            share = share + g_full[j]
        g_full[j] = share
        if h == len(cuts) - 1:
            z_send[j] = share.astype(BF16)

            @pl.when(j != z)
            def _():
                z_copy(j).start()

    before = None
    for h in range(len(cuts)):
        for i in range(n):
            relay(h, i)
            if before is not None:
                input_part(*before)
            before = (h, i)
    input_part(*before)

    all_tokens = tok[...].reshape(n * CORES * pair, width)
    for h, (low, high) in enumerate(cuts):
        full = lax.dot_general(
            all_tokens, slope[h][...].reshape(n * CORES * pair, high - low),
            (((0,), (0,)), ((), ())), preferred_element_type=F32,
        )
        for r in range(row_blocks):
            for c in range(low // block, high // block):
                wg_full[r * col_blocks + c] = full[
                    r * block:(r + 1) * block, c * block - low:(c + 1) * block - low
                ]
    for s in range(slots):
        live = jnp.where(s < count, 1, 0).astype(F32)
        w_grad[s] = (wg_full[places[s]] * live).astype(BF16)
    out_wg = pltpu.make_async_copy(w_grad, wg_ref.at[0, 0], lsem.at[5])
    out_wg.start()

    d_send[...] = g_full[z].reshape(CORES, X_HI, slab, width)
    for o in steps:
        source = z_other(o)

        @pl.when(source != z)
        def _():
            remote(z_send.at[0], z_recv.at[source], d1 + source, d1 + source, at_z(source)).wait_recv()
            d_send[...] += z_recv[source].astype(F32).reshape(CORES, X_HI, slab, width)

    d_copies = []
    for e in range(1, X_LO):
        to = turn(x_lo, e, X_LO)
        copy = remote(d_send.at[lax.rem(to, CORES), to // CORES], d_recv.at[e], d2 + e, d2 + e, at_x(to))
        copy.start()
        d_copies.append(copy)
        sends.append(copy)
    result = d_send[my_core, my_pair]
    for e in range(1, X_LO):
        d_copies[e - 1].wait_recv()
        result = result + d_recv[e]
    in_grad[...] = result.astype(BF16)
    out_ig = pltpu.make_async_copy(in_grad, ig_ref, lsem.at[6])
    out_ig.start()
    for copy in (out_act, out_wg, out_ig):
        copy.wait()

    for copy in sends:
        copy.wait_send()
    for e in range(1, n):
        to = turn(z, e, n)
        remote(tok.at[z], tok.at[z], az + to, az + z, at_z(to)).wait_send()
        z_copy(to).wait_send()
        to = turn(y, e, n)
        for h in range(len(cuts)):
            y_copy(h, 0, to).wait_send()
            here = slope[h].at[y, core]
            remote(here, here, c2[h] + to, c2[h] + y, at_y(to)).wait_send()
    for h in range(len(cuts)):
        for i in range(n):
            half_copy(h, i).wait_send()
            there = slope[h].at[i, core]
            remote(there, there, c3[h] + i, c3[h] + i, sibling).wait_send()


def store(act_ref, ig_ref, wg_ref, act_out, ig_out, wg_out, sem):
    copies = [
        pltpu.make_async_copy(wg_ref, wg_out, sem.at[0]),
        pltpu.make_async_copy(act_ref, act_out, sem.at[1]),
        pltpu.make_async_copy(ig_ref, ig_out, sem.at[2]),
    ]
    for copy in copies:
        copy.start()
    for copy in copies:
        copy.wait()


def on_device(ring, tokens, w_packed, kept_rows, kept_cols, kept_count, grad_act):
    n = ring
    block, slots = w_packed.shape[-1], w_packed.shape[2]
    slab, width = tokens.shape
    hidden_width = grad_act.shape[1]
    row_blocks, col_blocks = width // block, hidden_width // block
    pair = X_HI * slab
    middle = (col_blocks + 1) // 2 * block
    cuts = ((0, middle), (middle, hidden_width))
    sems = 2 * X_LO + 1 + 2 * n + len(cuts) * (4 * n + 1)
    vmem, smem = pl.BlockSpec(memory_space=pltpu.VMEM), pl.BlockSpec(memory_space=pltpu.SMEM)
    hbm = pl.BlockSpec(memory_space=pltpu.HBM)

    def each(lead, kind):
        return [pltpu.VMEM(lead + (high - low,), kind) for low, high in cuts]

    results = pl.pallas_call(
        functools.partial(kernel, n, row_blocks, col_blocks, cuts),
        out_shape=(
            jax.ShapeDtypeStruct(grad_act.shape, BF16),
            jax.ShapeDtypeStruct(tokens.shape, BF16),
            jax.ShapeDtypeStruct(w_packed.shape, BF16),
        ),
        in_specs=[smem, smem, hbm, hbm, hbm, hbm],
        out_specs=(hbm, hbm, hbm),
        scratch_shapes=[
            pltpu.VMEM((n, CORES, X_HI, slab, width), BF16),
            pltpu.VMEM((width, hidden_width), BF16),
            pltpu.VMEM((hidden_width, width), BF16),
            pltpu.VMEM((slots, block, block), BF16),
            pltpu.VMEM((X_HI, slab, hidden_width), BF16),
            pltpu.VMEM((X_HI, slab, hidden_width), BF16),
            pltpu.VMEM((n, CORES * pair, width), F32),
            pltpu.VMEM((n, CORES * pair, width), BF16),
            pltpu.VMEM((n, CORES * pair, width), BF16),
            pltpu.VMEM((CORES, X_HI, slab, width), F32),
            pltpu.VMEM((X_LO, slab, width), F32),
            pltpu.VMEM((row_blocks * col_blocks, block, block), F32),
            pltpu.VMEM((slots, block, block), BF16),
            pltpu.VMEM((slab, width), BF16),
            pltpu.SMEM((1, 1), jnp.int32),
            pltpu.SemaphoreType.DMA((sems,)),
            pltpu.SemaphoreType.DMA((sems,)),
            pltpu.SemaphoreType.DMA((7,)),
            *each((n, CORES, pair), F32),
            *each((n, pair), F32),
            *each((pair,), F32),
            *each((n, pair), BF16),
            *each((n, pair), BF16),
            *each((pair,), BF16),
            *each((pair,), BF16),
            *each((n, CORES, X_HI, slab), BF16),
        ],
        compiler_params=pltpu.CompilerParams(
            collective_id=0, has_side_effects=True
        ),
    )(kept_rows, kept_cols, kept_count, tokens, w_packed, grad_act)
    return tuple(pl.pallas_call(
        store,
        out_shape=tuple(jax.ShapeDtypeStruct(r.shape, r.dtype) for r in results),
        in_specs=[vmem] * 3,
        out_specs=(hbm,) * 3,
        scratch_shapes=[pltpu.SemaphoreType.DMA((3,))],
    )(*results))


def solution(mesh):
    ring = mesh.shape["row"] // (CORES * X_HI)
    placed = (
        P("col", "row"),
        P("row", "col", None, None, None),
        P("row", "col", None),
        P("row", "col", None),
        P("row", "col"),
        P("row", "col"),
    )
    return jax.shard_map(
        functools.partial(on_device, ring),
        mesh=mesh,
        in_specs=placed,
        out_specs=(P("row", "col"), P("col", "row"), P("row", "col", None, None, None)),
        check_vma=False,
    )
```

```python
import functools

import jax
import jax.numpy as jnp
from jax import lax
from jax.experimental import pallas as pl
from jax.experimental.pallas import tpu as pltpu
from jax.sharding import PartitionSpec as P

MESH = pl.DeviceIdType.MESH
BF16, F32 = jnp.bfloat16, jnp.float32

gelu_scale = 0.7978845608
gelu_cubic = 0.044715

X_LO = 4
X_HI = 2
CORES = 2


def gelu_pair(hidden, cotangent):
    inner = gelu_scale * (hidden + gelu_cubic * hidden * hidden * hidden)
    tangent = jnp.tanh(inner)
    activation = (0.5 * hidden * (1.0 + tangent)).astype(BF16)
    slope = 0.5 * (1.0 + tangent) + 0.5 * hidden * (1.0 - tangent * tangent) * gelu_scale * (
        1.0 + 3.0 * gelu_cubic * hidden * hidden
    )
    return activation, (cotangent.astype(F32) * slope).astype(BF16)


def kernel(
    ring, row_blocks, col_blocks, cuts,
    rows_ref, cols_ref, count_hbm, tokens_ref, w_hbm, gact_ref,
    act_ref, ig_ref, wg_ref,
    tok, dense, dense_t, w_ref, gpair, acts, g_full, z_send, z_recv, d_send, d_recv, wg_full, w_grad, in_grad, count_ref,
    ssem, rsem, lsem, *per_cut,
):
    n = ring
    part, sib, own, y_send, y_recv, x_send, x_recv, slope = (
        per_cut[i * len(cuts):(i + 1) * len(cuts)] for i in range(8)
    )
    row, col = lax.axis_index("row"), lax.axis_index("col")
    core, x_hi, y = lax.rem(row, CORES), lax.rem(row // CORES, X_HI), row // (CORES * X_HI)
    x_lo, z = lax.rem(col, X_LO), col // X_LO
    slots, block = w_ref.shape[0], w_ref.shape[1]
    width = row_blocks * block
    slab = tokens_ref.shape[0]
    pair = X_HI * slab

    def at_y(other):
        return ((other * X_HI + x_hi) * CORES + core, col)

    def at_z(other):
        return (row, other * X_LO + x_lo)

    def at_x(other):
        return (row, z * X_LO + other)

    sibling = ((y * X_HI + x_hi) * CORES + 1 - core, col)
    partner = ((y * X_HI + 1 - x_hi) * CORES + core, col)

    def turn(base, step, size):
        return lax.rem(base + step + size, size)

    barrier = pltpu.get_barrier_semaphore()
    peers = [sibling, partner]
    peers += [at_x(turn(x_lo, e, X_LO)) for e in range(1, X_LO)]
    peers += [at_z(turn(z, e, n)) for e in range(1, n)]
    peers += [at_y(turn(y, e, n)) for e in range(1, n)]
    for peer in peers:
        pl.semaphore_signal(barrier, inc=1, device_id=peer, device_id_type=MESH)

    used = [0]

    def numbers(size):
        used[0] += size
        return used[0] - size

    def remote(src, dst, send, receive, peer):
        return pltpu.make_async_remote_copy(
            src_ref=src, dst_ref=dst, send_sem=ssem.at[send], recv_sem=rsem.at[receive],
            device_id=peer, device_id_type=MESH,
        )

    steps = [i // 2 + (i % 2) * (n // 2) for i in range(n)]

    def piece(o):
        return lax.rem(y + z + o, n)

    def y_other(o):
        return lax.rem(y - z - o + 2 * n, n)

    def z_other(o):
        return lax.rem(z - y - o + 2 * n, n)

    my_core, my_pair = lax.rem(x_lo, CORES), x_lo // CORES
    mine = tok.at[z, my_core, my_pair]
    local = [
        pltpu.make_async_copy(tokens_ref, mine, lsem.at[0]),
        pltpu.make_async_copy(w_hbm.at[0, 0], w_ref, lsem.at[1]),
        pltpu.make_async_copy(count_hbm, count_ref, lsem.at[2]),
        pltpu.make_async_copy(gact_ref, gpair.at[x_hi], lsem.at[3]),
    ]
    for copy in local:
        copy.start()
    local[0].wait()
    pl.semaphore_wait(barrier, len(peers))

    sends = []
    ax = numbers(X_LO)
    for e in range(1, X_LO):
        copy = remote(mine, mine, ax + e, ax + e, at_x(turn(x_lo, e, X_LO)))
        copy.start()
        sends.append(copy)

    for e in range(1, X_LO):
        source = turn(x_lo, -e, X_LO)
        theirs = tok.at[z, lax.rem(source, CORES), source // CORES]
        remote(theirs, theirs, ax + e, ax + e, at_x(source)).wait_recv()
    az = numbers(n)
    for o in steps:
        to = z_other(o)

        @pl.when(to != z)
        def _():
            remote(tok.at[z], tok.at[z], az + to, az + z, at_z(to)).start()

    for copy in local[1:]:
        copy.wait()
    gp = numbers(1)
    gp_copy = remote(gpair.at[x_hi], gpair.at[x_hi], gp, gp, partner)
    gp_copy.start()
    sends.append(gp_copy)
    count = count_ref[0, 0]
    places = [rows_ref[0, 0, s] * col_blocks + cols_ref[0, 0, s] for s in range(slots)]
    for p in range(row_blocks * col_blocks):
        slot = jnp.int32(0)
        for s in range(slots):
            slot = jnp.where(places[s] == p, s, slot)
        live = jnp.where(slot < count, 1, 0).astype(F32)
        r, c = p // col_blocks, p % col_blocks
        dense[r * block:(r + 1) * block, c * block:(c + 1) * block] = (
            w_ref[slot].astype(F32) * live
        ).astype(BF16)
        dense_t[c * block:(c + 1) * block, r * block:(r + 1) * block] = jnp.transpose(
            w_ref[slot].astype(F32) * live
        ).astype(BF16)

    b1 = [numbers(n) for _ in cuts]
    b2 = [numbers(n) for _ in cuts]
    b3 = [numbers(1) for _ in cuts]
    c2 = [numbers(n) for _ in cuts]
    c3 = [numbers(n) for _ in cuts]
    d1, d2 = numbers(n), numbers(X_LO)

    def half_copy(h, i):
        return remote(part[h].at[i, 1 - core], sib[h].at[i], b1[h] + i, b1[h] + i, sibling)

    def y_copy(h, i, to):
        return remote(y_send[h].at[i], y_recv[h].at[y], b2[h] + to, b2[h] + y, at_y(to))

    def multiply(h, i):
        low, high = cuts[h]
        j = piece(steps[i])
        if h == 0:
            @pl.when(j != z)
            def _():
                remote(tok.at[j], tok.at[j], az + j, az + j, at_z(j)).wait_recv()
        product = jnp.dot(
            tok[j].reshape(CORES * pair, width), dense[:, low:high], preferred_element_type=F32
        )
        part[h][i] = product.reshape(CORES, pair, high - low)
        half_copy(h, i).start()

    def pass_on(h, i):
        j = piece(steps[i])
        half_copy(h, i).wait_recv()
        both = part[h][i, core] + sib[h][i]
        y_send[h][i] = both.astype(BF16)

        @pl.when(j == y)
        def _():
            own[h][...] = both

        @pl.when(j != y)
        def _():
            y_copy(h, i, j).start()

    before = None
    for h in range(len(cuts)):
        for i in range(n):
            multiply(h, i)
            if before is not None:
                pass_on(*before)
            before = (h, i)
    pass_on(*before)

    for h, (low, high) in enumerate(cuts):
        for o in steps:
            source = y_other(o)

            @pl.when(source != y)
            def _():
                remote(
                    y_send[h].at[0], y_recv[h].at[source], b2[h] + source, b2[h] + source, at_y(source)
                ).wait_recv()
                own[h][...] += y_recv[h][source].astype(F32)

        x_send[h][...] = own[h][...].astype(BF16)
        x_copy = remote(x_send[h], x_recv[h], b3[h], b3[h], partner)
        x_copy.start()
        sends.append(x_copy)
        x_copy.wait_recv()
        if h == 0:
            gp_copy.wait_recv()
        hidden = own[h][...] + x_recv[h][...].astype(F32)
        activation, grad = gelu_pair(hidden, gpair[:, :, low:high].reshape(pair, high - low))
        acts[:, :, low:high] = activation.reshape(X_HI, slab, high - low)
        slope[h][y, core] = grad.reshape(X_HI, slab, high - low)

        for o in steps:
            to = y_other(o)

            @pl.when(to != y)
            def _():
                here = slope[h].at[y, core]
                remote(here, here, c2[h] + to, c2[h] + y, at_y(to)).start()

        here = slope[h].at[y, core]
        remote(here, here, c3[h] + y, c3[h] + y, sibling).start()
    out_act = pltpu.make_async_copy(acts.at[x_hi], act_ref, lsem.at[4])
    out_act.start()

    def z_copy(to):
        return remote(z_send.at[to], z_recv.at[z], d1 + to, d1 + z, at_z(to))

    near_first = sorted(range(n), key=lambda d: (min(d, n - d), d))

    def arrival(h, i):
        return turn(y, -near_first[i], n)

    def relay(h, i):
        j = arrival(h, i)

        @pl.when(j != y)
        def _():
            there = slope[h].at[j, core]
            remote(there, there, c2[h] + j, c2[h] + j, at_y(j)).wait_recv()
            remote(there, there, c3[h] + j, c3[h] + j, sibling).start()

    def input_part(h, i):
        low, high = cuts[h]
        j = arrival(h, i)
        there = slope[h].at[j, 1 - core]
        remote(there, there, c3[h] + j, c3[h] + j, sibling).wait_recv()
        share = jnp.dot(
            slope[h][j].reshape(CORES * pair, high - low), dense_t[low:high], preferred_element_type=F32
        )
        if h:
            share = share + g_full[j]
        g_full[j] = share
        if h == len(cuts) - 1:
            z_send[j] = share.astype(BF16)

            @pl.when(j != z)
            def _():
                z_copy(j).start()

    before = None
    for h in range(len(cuts)):
        for i in range(n):
            relay(h, i)
            if before is not None:
                input_part(*before)
            before = (h, i)
    input_part(*before)

    all_tokens = tok[...].reshape(n * CORES * pair, width)
    for h, (low, high) in enumerate(cuts):
        full = lax.dot_general(
            all_tokens, slope[h][...].reshape(n * CORES * pair, high - low),
            (((0,), (0,)), ((), ())), preferred_element_type=F32,
        )
        for r in range(row_blocks):
            for c in range(low // block, high // block):
                wg_full[r * col_blocks + c] = full[
                    r * block:(r + 1) * block, c * block - low:(c + 1) * block - low
                ]
    for s in range(slots):
        live = jnp.where(s < count, 1, 0).astype(F32)
        w_grad[s] = (wg_full[places[s]] * live).astype(BF16)
    out_wg = pltpu.make_async_copy(w_grad, wg_ref.at[0, 0], lsem.at[5])
    out_wg.start()

    d_send[...] = g_full[z].reshape(CORES, X_HI, slab, width)
    for o in steps:
        source = z_other(o)

        @pl.when(source != z)
        def _():
            remote(z_send.at[0], z_recv.at[source], d1 + source, d1 + source, at_z(source)).wait_recv()
            d_send[...] += z_recv[source].astype(F32).reshape(CORES, X_HI, slab, width)

    d_copies = []
    for e in range(1, X_LO):
        to = turn(x_lo, e, X_LO)
        copy = remote(d_send.at[lax.rem(to, CORES), to // CORES], d_recv.at[e], d2 + e, d2 + e, at_x(to))
        copy.start()
        d_copies.append(copy)
        sends.append(copy)
    result = d_send[my_core, my_pair]
    for e in range(1, X_LO):
        d_copies[e - 1].wait_recv()
        result = result + d_recv[e]
    in_grad[...] = result.astype(BF16)
    out_ig = pltpu.make_async_copy(in_grad, ig_ref, lsem.at[6])
    out_ig.start()
    for copy in (out_act, out_wg, out_ig):
        copy.wait()

    for copy in sends:
        copy.wait_send()
    for e in range(1, n):
        to = turn(z, e, n)
        remote(tok.at[z], tok.at[z], az + to, az + z, at_z(to)).wait_send()
        z_copy(to).wait_send()
        to = turn(y, e, n)
        for h in range(len(cuts)):
            y_copy(h, 0, to).wait_send()
            here = slope[h].at[y, core]
            remote(here, here, c2[h] + to, c2[h] + y, at_y(to)).wait_send()
    for h in range(len(cuts)):
        for i in range(n):
            half_copy(h, i).wait_send()
            there = slope[h].at[i, core]
            remote(there, there, c3[h] + i, c3[h] + i, sibling).wait_send()


def store(act_ref, ig_ref, wg_ref, act_out, ig_out, wg_out, sem):
    copies = [
        pltpu.make_async_copy(wg_ref, wg_out, sem.at[0]),
        pltpu.make_async_copy(act_ref, act_out, sem.at[1]),
        pltpu.make_async_copy(ig_ref, ig_out, sem.at[2]),
    ]
    for copy in copies:
        copy.start()
    for copy in copies:
        copy.wait()


def on_device(ring, tokens, w_packed, kept_rows, kept_cols, kept_count, grad_act):
    n = ring
    block, slots = w_packed.shape[-1], w_packed.shape[2]
    slab, width = tokens.shape
    hidden_width = grad_act.shape[1]
    row_blocks, col_blocks = width // block, hidden_width // block
    pair = X_HI * slab
    middle = (col_blocks + 1) // 2 * block
    cuts = ((0, middle), (middle, hidden_width))
    sems = 2 * X_LO + 1 + 2 * n + len(cuts) * (4 * n + 1)
    vmem, smem = pl.BlockSpec(memory_space=pltpu.VMEM), pl.BlockSpec(memory_space=pltpu.SMEM)
    hbm = pl.BlockSpec(memory_space=pltpu.HBM)

    def each(lead, kind):
        return [pltpu.VMEM(lead + (high - low,), kind) for low, high in cuts]

    results = pl.pallas_call(
        functools.partial(kernel, n, row_blocks, col_blocks, cuts),
        out_shape=(
            jax.ShapeDtypeStruct(grad_act.shape, BF16),
            jax.ShapeDtypeStruct(tokens.shape, BF16),
            jax.ShapeDtypeStruct(w_packed.shape, BF16),
        ),
        in_specs=[smem, smem, hbm, hbm, hbm, hbm],
        out_specs=(hbm, hbm, hbm),
        scratch_shapes=[
            pltpu.VMEM((n, CORES, X_HI, slab, width), BF16),
            pltpu.VMEM((width, hidden_width), BF16),
            pltpu.VMEM((hidden_width, width), BF16),
            pltpu.VMEM((slots, block, block), BF16),
            pltpu.VMEM((X_HI, slab, hidden_width), BF16),
            pltpu.VMEM((X_HI, slab, hidden_width), BF16),
            pltpu.VMEM((n, CORES * pair, width), F32),
            pltpu.VMEM((n, CORES * pair, width), BF16),
            pltpu.VMEM((n, CORES * pair, width), BF16),
            pltpu.VMEM((CORES, X_HI, slab, width), F32),
            pltpu.VMEM((X_LO, slab, width), F32),
            pltpu.VMEM((row_blocks * col_blocks, block, block), F32),
            pltpu.VMEM((slots, block, block), BF16),
            pltpu.VMEM((slab, width), BF16),
            pltpu.SMEM((1, 1), jnp.int32),
            pltpu.SemaphoreType.DMA((sems,)),
            pltpu.SemaphoreType.DMA((sems,)),
            pltpu.SemaphoreType.DMA((7,)),
            *each((n, CORES, pair), F32),
            *each((n, pair), F32),
            *each((pair,), F32),
            *each((n, pair), BF16),
            *each((n, pair), BF16),
            *each((pair,), BF16),
            *each((pair,), BF16),
            *each((n, CORES, X_HI, slab), BF16),
        ],
        compiler_params=pltpu.CompilerParams(
            collective_id=0, has_side_effects=True
        ),
    )(kept_rows, kept_cols, kept_count, tokens, w_packed, grad_act)
    return tuple(pl.pallas_call(
        store,
        out_shape=tuple(jax.ShapeDtypeStruct(r.shape, r.dtype) for r in results),
        in_specs=[vmem] * 3,
        out_specs=(hbm,) * 3,
        scratch_shapes=[pltpu.SemaphoreType.DMA((3,))],
    )(*results))


def solution(mesh):
    ring = mesh.shape["row"] // (CORES * X_HI)
    placed = (
        P("col", "row"),
        P("row", "col", None, None, None),
        P("row", "col", None),
        P("row", "col", None),
        P("row", "col"),
        P("row", "col"),
    )
    return jax.shard_map(
        functools.partial(on_device, ring),
        mesh=mesh,
        in_specs=placed,
        out_specs=(P("row", "col"), P("col", "row"), P("row", "col", None, None, None)),
        check_vma=False,
    )
```
